32 devices in a mesh: fsdp: 4 (over z), ctx: 4 (over y, core), tp: 2 (over x).
Axes of the slice: x: 2, y: 2, z: 4, core: 2. Of those that a mesh axis runs over, the one named last changes fastest.
Arguments:
- tokens: bfloat16 [4, 1024, 1024], P('fsdp', 'ctx'), may hold values from -6 to 6
- cotangent: bfloat16 [4, 1024, 1024], P('fsdp', 'ctx'), may hold values from -6 to 6
- ln1_gain: bfloat16 [1024], P('fsdp'), may hold values from 0.5 to 1.5
- ln1_bias: bfloat16 [1024], P('fsdp'), may hold values from -1.5 to 1.5
- qkv_weight: bfloat16 [1024, 3, 1024], P('fsdp', None, 'tp'), may hold values from -4 to 4
- qv_bias: bfloat16 [2, 1024], P(None, ('tp', 'fsdp')), may hold values from -1.5 to 1.5
- out_weight: bfloat16 [1024, 1024], P('tp', 'fsdp'), may hold values from -2 to 2
- out_bias: bfloat16 [1024], P('fsdp'), may hold values from -1.5 to 1.5
- ln2_gain: bfloat16 [1024], P('fsdp'), may hold values from 0.5 to 1.5
- ln2_bias: bfloat16 [1024], P('fsdp'), may hold values from -1.5 to 1.5
- fc_weight: bfloat16 [1024, 4096], P('fsdp', 'tp'), may hold values from -0.1875 to 0.1875
- fc_bias: bfloat16 [4096], P(('tp', 'fsdp')), may hold values from -1.5 to 1.5
- proj_weight: bfloat16 [4096, 1024], P('tp', 'fsdp'), may hold values from -0.09375 to 0.09375
- proj_bias: bfloat16 [1024], P('fsdp'), may hold values from -1.5 to 1.5
Outputs:
- layer_out: bfloat16 [4, 1024, 1024], P('fsdp', 'ctx')
- grad_input: bfloat16 [4, 1024, 1024], P('fsdp', 'ctx')
- grad_ln1_gain: float32 [1024], P('fsdp')
- grad_ln1_bias: float32 [1024], P('fsdp')
- grad_qkv_weight: float32 [1024, 3, 1024], P('fsdp', None, 'tp')
- grad_qv_bias: float32 [2, 1024], P(None, ('tp', 'fsdp'))
- grad_out_weight: float32 [1024, 1024], P('tp', 'fsdp')
- grad_out_bias: float32 [1024], P('fsdp')
- grad_ln2_gain: float32 [1024], P('fsdp')
- grad_ln2_bias: float32 [1024], P('fsdp')
- grad_fc_weight: float32 [1024, 4096], P('fsdp', 'tp')
- grad_fc_bias: float32 [4096], P(('tp', 'fsdp'))
- grad_proj_weight: float32 [4096, 1024], P('tp', 'fsdp')
- grad_proj_bias: float32 [1024], P('fsdp')
The draws below stay inside these ranges and needn't reach their ends.
All inputs are finite; a program needn't handle non-finite values.
Results may differ from the reference program's by a relative error of at most 0.02.
Values may be sent and summed in bfloat16 or wider, within the bound.
A program may use at most 128 MiB of HBM per device.

```python
import math
import jax
import jax.numpy as jnp
from jax import lax

D = 1024
H = 16
HD = 64
FF = 4096
LEN = 1024
SEQS = 4


def draw_qkv_weight(key, part):
    base = jnp.clip(jax.random.normal(key, (D, 3, D), jnp.float32), -5.0, 5.0) * D ** (-0.5)
    return base.astype(jnp.bfloat16)


def levels(key, dims, pieces, least, high):
    factor_of = 1.0
    for axis_at, shards_of in pieces:
        draws = jax.random.uniform(jax.random.fold_in(jax.random.fold_in(key, 6), axis_at), (shards_of,), jnp.float32, least / len(pieces), high / len(pieces))
        factor_of = factor_of * jnp.repeat(jnp.exp(draws), dims[axis_at] // shards_of).reshape((-1,) + (1,) * (len(dims) - 1 - axis_at))
    return factor_of


def gaussian(stream_key, dims, deviation, most, pieces=(), kind=jnp.bfloat16):
    gain = levels(stream_key, dims, pieces, -0.22, 0.18) if pieces else 1.0
    result = jax.random.normal(stream_key, dims, jnp.float32) * deviation * gain
    return jnp.minimum(jnp.maximum(result, -most), most).astype(kind)


def setup_inputs(seed: int = 0) -> dict:
    streams_of = jax.random.split(jax.random.key(seed), 15)
    return {
        "tokens": gaussian(streams_of[0], (SEQS, LEN, D), 1.0, 6.0, ((0, 4), (1, 4))),
        "cotangent": gaussian(streams_of[1], (SEQS, LEN, D), 1.0, 6.0, ((0, 4), (1, 4))),
        "ln1_gain": jnp.clip(1.0 + 0.1 * jax.random.normal(streams_of[2], (D,), jnp.float32), 0.5, 1.5).astype(jnp.bfloat16),
        "ln1_bias": gaussian(streams_of[3], (D,), 0.3, 1.5, ((0, 4),)),
        "qkv_weight": draw_qkv_weight(jax.random.fold_in(streams_of[14], 71), 0),
        "qv_bias": gaussian(streams_of[5], (2, D), 0.3, 1.5, ((1, 8),)),
        "out_weight": gaussian(streams_of[6], (D, D), (D * 8 // LEN) ** -0.5, 2.0, ((0, 2), (1, 4))),
        "out_bias": gaussian(streams_of[7], (D,), 0.3, 1.5, ((0, 4),)),
        "ln2_gain": jnp.clip(1.0 + 0.1 * jax.random.normal(streams_of[8], (D,), jnp.float32), 0.5, 1.5).astype(jnp.bfloat16),
        "ln2_bias": gaussian(streams_of[9], (D,), 0.3, 1.5, ((0, 4),)),
        "fc_weight": gaussian(streams_of[10], (D, FF), D ** -0.5, 0.1875, ((0, 4), (1, 2))),
        "fc_bias": gaussian(streams_of[11], (FF,), 0.3, 1.5, ((0, 8),)),
        "proj_weight": gaussian(streams_of[12], (FF, D), FF ** -0.5, 0.09375, ((0, 2), (1, 4))),
        "proj_bias": gaussian(streams_of[13], (D,), 0.3, 1.5, ((0, 4),)),
    }


EPSILON = 1e-05
GELU_COEF = math.sqrt(2.0 / math.pi)
MASK_FILL = -1e+30

def contract(form, left, right):
    return jnp.einsum(form, left.astype(jnp.float32), right.astype(jnp.float32))

def norm_forward(values):
    centre = lax.optimization_barrier(jnp.mean(values, axis=-1, keepdims=True))
    centred = values - centre
    inverse = lax.rsqrt(lax.optimization_barrier(jnp.mean(centred * centred, axis=-1, keepdims=True)) + EPSILON)
    return (centred * inverse, inverse)

def norm_backward(upstream, normed, inverse, gain_full):
    scaled = upstream * gain_full
    first = lax.optimization_barrier(jnp.mean(scaled, axis=-1, keepdims=True))
    second = lax.optimization_barrier(jnp.mean(scaled * normed, axis=-1, keepdims=True))
    return inverse * (scaled - first - normed * second)

def gelu_parts(pre_act):
    cubic = pre_act * pre_act * pre_act
    tangent = jnp.tanh(GELU_COEF * (pre_act + 0.044715 * cubic))
    value_out = 0.5 * pre_act * (1.0 + tangent)
    slope_out = 0.5 * (1.0 + tangent) + 0.5 * pre_act * (1.0 - tangent * tangent) * GELU_COEF * (1.0 + 3.0 * 0.044715 * pre_act * pre_act)
    return (value_out, slope_out)

def causal_scores(query_block, key_heads, start_row):
    block_rows = query_block.shape[1]
    length = key_heads.shape[1]
    score_scale = query_block.shape[2] ** (-0.5)
    scores = contract('gqe,gke->gqk', query_block, key_heads) * score_scale
    query_pos = start_row + jnp.arange(block_rows, dtype=jnp.int32)
    key_pos = jnp.arange(length, dtype=jnp.int32)
    allowed = key_pos[None, :] <= query_pos[:, None]
    return jnp.where(allowed[None], scores, MASK_FILL)

def attend(query_heads, key_heads, value_heads):
    groups, length, depth = query_heads.shape
    block_rows = min(512, length)
    block_count = length // block_rows

    def one_block(block_index):
        start_row = block_index * block_rows
        query_block = lax.dynamic_slice_in_dim(query_heads, start_row, block_rows, 1)
        scores = causal_scores(query_block, key_heads, start_row)
        row_max = lax.optimization_barrier(jnp.max(scores, axis=-1, keepdims=True))
        log_total = row_max[..., 0] + jnp.log(lax.optimization_barrier(jnp.sum(jnp.exp(scores - row_max), axis=-1)))
        soft_weights = jnp.exp(scores - log_total[..., None]).astype(jnp.bfloat16)
        block_out = contract('gqk,gke->gqe', soft_weights, value_heads).astype(jnp.bfloat16)
        return (block_out, log_total)
    outputs, totals = lax.map(one_block, jnp.arange(block_count, dtype=jnp.int32))
    outputs = outputs.transpose(1, 0, 2, 3).reshape(groups, length, depth)
    totals = totals.transpose(1, 0, 2).reshape(groups, length)
    return (outputs, totals)

def attend_back(query_heads, key_heads, value_heads, output_heads, log_total, grad_heads):
    groups, length, depth = query_heads.shape
    block_rows = min(512, length)
    block_count = length // block_rows
    score_scale = depth ** (-0.5)

    def one_block(carried, block_index):
        grad_keys, grad_values = carried
        start_row = block_index * block_rows
        query_block = lax.dynamic_slice_in_dim(query_heads, start_row, block_rows, 1)
        output_block = lax.dynamic_slice_in_dim(output_heads, start_row, block_rows, 1)
        grad_block = lax.dynamic_slice_in_dim(grad_heads, start_row, block_rows, 1)
        total_block = lax.dynamic_slice_in_dim(log_total, start_row, block_rows, 1)
        scores = causal_scores(query_block, key_heads, start_row)
        soft_full = jnp.exp(scores - total_block[..., None])
        soft_low = soft_full.astype(jnp.bfloat16)
        grad_values = grad_values + contract('gqk,gqe->gke', soft_low, grad_block)
        grad_soft = contract('gqe,gke->gqk', grad_block, value_heads)
        diagonal = lax.optimization_barrier(jnp.sum(grad_block.astype(jnp.float32) * output_block.astype(jnp.float32), axis=-1))
        grad_scores = (soft_full * (grad_soft - diagonal[..., None]) * score_scale).astype(jnp.bfloat16)
        grad_query = contract('gqk,gke->gqe', grad_scores, key_heads)
        grad_keys = grad_keys + contract('gqk,gqe->gke', grad_scores, query_block)
        return ((grad_keys, grad_values), grad_query)
    zero_heads = jnp.zeros((groups, length, depth), jnp.float32)
    (grad_keys, grad_values), grad_queries = lax.scan(one_block, (zero_heads, zero_heads), jnp.arange(block_count, dtype=jnp.int32))
    grad_queries = grad_queries.transpose(1, 0, 2, 3).reshape(groups, length, depth)
    return (grad_queries, grad_keys, grad_values)

def layer_sequence(inputs, upstream, params):
    gain_one, bias_one, weight_qkv, bias_qv, weight_out, bias_out, gain_two, bias_two, weight_fc, bias_fc, weight_proj, bias_proj = params
    length, width = inputs.shape
    inputs_full = inputs.astype(jnp.float32)
    gain_one_f = gain_one.astype(jnp.float32)
    gain_two_f = gain_two.astype(jnp.float32)
    normed_one, inv_one = norm_forward(inputs_full)
    hidden_one = (normed_one * gain_one_f + bias_one.astype(jnp.float32)).astype(jnp.bfloat16)
    qkv_full = contract('td,dcf->ctf', hidden_one, weight_qkv)
    zero_row = jnp.zeros((width,), jnp.float32)
    bias_three = jnp.stack([bias_qv[0].astype(jnp.float32), zero_row, bias_qv[1].astype(jnp.float32)])
    qkv_low = (qkv_full + bias_three[:, None, :]).astype(jnp.bfloat16)
    head_view = qkv_low.reshape(3, length, H, HD).transpose(0, 2, 1, 3)
    heads_out, log_total = attend(head_view[0], head_view[1], head_view[2])
    heads_rows = heads_out.transpose(1, 0, 2).reshape(length, width)
    mid = inputs_full + jnp.dot(heads_rows, weight_out, preferred_element_type=jnp.float32) + bias_out.astype(jnp.float32)
    normed_two, inv_two = norm_forward(mid)
    hidden_two = (normed_two * gain_two_f + bias_two.astype(jnp.float32)).astype(jnp.bfloat16)
    pre_act = jnp.dot(hidden_two, weight_fc, preferred_element_type=jnp.float32) + bias_fc.astype(jnp.float32)
    act_full, act_slope = gelu_parts(pre_act)
    act_low = act_full.astype(jnp.bfloat16)
    layer_out = (mid + jnp.dot(act_low, weight_proj, preferred_element_type=jnp.float32) + bias_proj.astype(jnp.float32)).astype(jnp.bfloat16)
    upstream_full = upstream.astype(jnp.float32)
    grad_proj_weight = contract('tf,td->fd', act_low, upstream)
    grad_proj_bias = lax.optimization_barrier(jnp.sum(upstream_full, axis=0))
    grad_pre = contract('td,fd->tf', upstream, weight_proj) * act_slope
    grad_pre_low = grad_pre.astype(jnp.bfloat16)
    grad_fc_bias = lax.optimization_barrier(jnp.sum(grad_pre, axis=0))
    grad_fc_weight = contract('td,tf->df', hidden_two, grad_pre_low)
    grad_hidden_two = contract('tf,df->td', grad_pre_low, weight_fc)
    grad_ln2_gain = lax.optimization_barrier(jnp.sum(grad_hidden_two * normed_two, axis=0))
    grad_ln2_bias = lax.optimization_barrier(jnp.sum(grad_hidden_two, axis=0))
    grad_mid = upstream_full + norm_backward(grad_hidden_two, normed_two, inv_two, gain_two_f)
    grad_mid_low = grad_mid.astype(jnp.bfloat16)
    grad_out_bias = lax.optimization_barrier(jnp.sum(grad_mid, axis=0))
    grad_out_weight = contract('tf,td->fd', heads_rows, grad_mid_low)
    grad_heads = contract('td,fd->tf', grad_mid_low, weight_out).astype(jnp.bfloat16)
    grad_head_view = grad_heads.reshape(length, H, HD).transpose(1, 0, 2)
    grad_queries, grad_keys, grad_values = attend_back(head_view[0], head_view[1], head_view[2], heads_out, log_total, grad_head_view)
    grad_qkv = jnp.stack([grad_queries, grad_keys, grad_values]).astype(jnp.bfloat16)
    grad_qkv = grad_qkv.transpose(0, 2, 1, 3).reshape(3, length, width)
    grad_qv_bias = jnp.stack([lax.optimization_barrier(jnp.sum(grad_qkv[0].astype(jnp.float32), axis=0)), lax.optimization_barrier(jnp.sum(grad_qkv[2].astype(jnp.float32), axis=0))])
    grad_qkv_weight = contract('td,ctf->dcf', hidden_one, grad_qkv)
    grad_hidden_one = contract('ctf,dcf->td', grad_qkv, weight_qkv)
    grad_ln1_gain = lax.optimization_barrier(jnp.sum(grad_hidden_one * normed_one, axis=0))
    grad_ln1_bias = lax.optimization_barrier(jnp.sum(grad_hidden_one, axis=0))
    grad_input = (grad_mid + norm_backward(grad_hidden_one, normed_one, inv_one, gain_one_f)).astype(jnp.bfloat16)
    grads = (grad_ln1_gain, grad_ln1_bias, grad_qkv_weight, grad_qv_bias, grad_out_weight, grad_out_bias, grad_ln2_gain, grad_ln2_bias, grad_fc_weight, grad_fc_bias, grad_proj_weight, grad_proj_bias)
    return (layer_out, grad_input, grads)

def reference(tokens, cotangent, ln1_gain, ln1_bias, qkv_weight, qv_bias, out_weight, out_bias, ln2_gain, ln2_bias, fc_weight, fc_bias, proj_weight, proj_bias):
    params = (ln1_gain, ln1_bias, qkv_weight, qv_bias, out_weight, out_bias, ln2_gain, ln2_bias, fc_weight, fc_bias, proj_weight, proj_bias)
    zero_grads = tuple((jnp.zeros(param.shape, jnp.float32) for param in params))

    def seq_step(running, seq_pair):
        layer_out, grad_input, grads = layer_sequence(seq_pair[0], seq_pair[1], params)
        return (jax.tree.map(lambda left, right: left + right, running, grads), (layer_out, grad_input))
    totals, (outputs, grad_inputs) = lax.scan(seq_step, zero_grads, (tokens, cotangent))
    return (outputs, grad_inputs, totals[0], totals[1], totals[2], totals[3], totals[4], totals[5], totals[6], totals[7], totals[8], totals[9], totals[10], totals[11])
```

```python
import math

import jax
import jax.numpy as jnp
from jax import lax
from jax.sharding import PartitionSpec as P

HD = 64


EPSILON = 1e-05
GELU_COEF = math.sqrt(2.0 / math.pi)
MASK_FILL = -1e30


def contract(form, left, right):
    return jnp.einsum(form, left, right, preferred_element_type=jnp.float32)


def norm_forward(values):
    centre = jnp.mean(values, axis=-1, keepdims=True)
    centred = values - centre
    inverse = lax.rsqrt(jnp.mean(centred * centred, axis=-1, keepdims=True) + EPSILON)
    return (centred * inverse, inverse)


def norm_backward(upstream, normed, inverse, gain_full):
    scaled = upstream * gain_full
    first = jnp.mean(scaled, axis=-1, keepdims=True)
    second = jnp.mean(scaled * normed, axis=-1, keepdims=True)
    return inverse * (scaled - first - normed * second)


def gelu_parts(pre_act):
    cubic = pre_act * pre_act * pre_act
    tangent = jnp.tanh(GELU_COEF * (pre_act + 0.044715 * cubic))
    value_out = 0.5 * pre_act * (1.0 + tangent)
    slope_out = 0.5 * (1.0 + tangent) + 0.5 * pre_act * (1.0 - tangent * tangent) * GELU_COEF * (
        1.0 + 3.0 * 0.044715 * pre_act * pre_act
    )
    return (value_out, slope_out)


def causal_scores(query_block, key_heads, start_row):
    block_rows = query_block.shape[1]
    length = key_heads.shape[1]
    score_scale = query_block.shape[2] ** (-0.5)
    scores = contract("gqe,gke->gqk", query_block, key_heads) * score_scale
    query_pos = start_row + jnp.arange(block_rows, dtype=jnp.int32)
    key_pos = jnp.arange(length, dtype=jnp.int32)
    allowed = key_pos[None, :] <= query_pos[:, None]
    return jnp.where(allowed[None], scores, MASK_FILL)


def attend(query_heads, key_heads, value_heads):
    groups, length, depth = query_heads.shape
    block_rows = min(512, length)
    block_count = length // block_rows

    def one_block(block_index):
        start_row = block_index * block_rows
        query_block = lax.dynamic_slice_in_dim(query_heads, start_row, block_rows, 1)
        scores = causal_scores(query_block, key_heads, start_row)
        row_max = jnp.max(scores, axis=-1, keepdims=True)
        log_total = row_max[..., 0] + jnp.log(jnp.sum(jnp.exp(scores - row_max), axis=-1))
        soft_weights = jnp.exp(scores - log_total[..., None]).astype(jnp.bfloat16)
        block_out = contract("gqk,gke->gqe", soft_weights, value_heads).astype(jnp.bfloat16)
        return (block_out, log_total)

    outputs, totals = lax.map(one_block, jnp.arange(block_count, dtype=jnp.int32))
    outputs = outputs.transpose(1, 0, 2, 3).reshape(groups, length, depth)
    totals = totals.transpose(1, 0, 2).reshape(groups, length)
    return (outputs, totals)


def attend_back(query_heads, key_heads, value_heads, output_heads, log_total, grad_heads):
    groups, length, depth = query_heads.shape
    block_rows = min(512, length)
    block_count = length // block_rows
    score_scale = depth ** (-0.5)

    def one_block(carried, block_index):
        grad_keys, grad_values = carried
        start_row = block_index * block_rows
        query_block = lax.dynamic_slice_in_dim(query_heads, start_row, block_rows, 1)
        output_block = lax.dynamic_slice_in_dim(output_heads, start_row, block_rows, 1)
        grad_block = lax.dynamic_slice_in_dim(grad_heads, start_row, block_rows, 1)
        total_block = lax.dynamic_slice_in_dim(log_total, start_row, block_rows, 1)
        scores = causal_scores(query_block, key_heads, start_row)
        soft_full = jnp.exp(scores - total_block[..., None])
        soft_low = soft_full.astype(jnp.bfloat16)
        grad_values = grad_values + contract("gqk,gqe->gke", soft_low, grad_block)
        grad_soft = contract("gqe,gke->gqk", grad_block, value_heads)
        diagonal = jnp.sum(
            grad_block.astype(jnp.float32) * output_block.astype(jnp.float32), axis=-1
        )
        grad_scores = (soft_full * (grad_soft - diagonal[..., None]) * score_scale).astype(
            jnp.bfloat16
        )
        grad_query = contract("gqk,gke->gqe", grad_scores, key_heads)
        grad_keys = grad_keys + contract("gqk,gqe->gke", grad_scores, query_block)
        return ((grad_keys, grad_values), grad_query)

    zero_heads = jnp.zeros((groups, length, depth), jnp.float32)
    (grad_keys, grad_values), grad_queries = lax.scan(
        one_block, (zero_heads, zero_heads), jnp.arange(block_count, dtype=jnp.int32)
    )
    grad_queries = grad_queries.transpose(1, 0, 2, 3).reshape(groups, length, depth)
    return (grad_queries, grad_keys, grad_values)


def own_part(values):
    rows = values.shape[0] // lax.axis_size("ctx")
    return lax.dynamic_slice_in_dim(values, lax.axis_index("ctx") * rows, rows, 0)


def gather_rows(shard):
    return lax.all_gather(own_part(shard), ("fsdp", "ctx"), axis=0, tiled=True)


def scatter_rows(grad):
    return lax.psum_scatter(
        grad.astype(jnp.bfloat16), ("fsdp", "ctx"), scatter_dimension=0, tiled=True
    )


def join_rows(part):
    members = lax.axis_size("ctx")
    if members & (members - 1):
        return lax.all_gather(part, "ctx", axis=0, tiled=True)
    place = lax.axis_index("ctx")
    rows, columns = part.shape
    held = part[None]
    step = members // 2
    while step:
        other = lax.ppermute(held, "ctx", [(i, i ^ step) for i in range(members)])
        upper = (place // step) % 2 == 1
        first = jnp.where(upper, other, held)
        second = jnp.where(upper, held, other)
        held = jnp.stack([first, second], axis=1).reshape(-1, rows, columns)
        step //= 2
    return held.reshape(members * rows, columns)


def pair_sum(values):
    if lax.axis_size("tp") == 2:
        other = lax.ppermute(values, "tp", [(0, 1), (1, 0)])
        return values.astype(jnp.float32) + other.astype(jnp.float32)
    return lax.psum(values, "tp").astype(jnp.float32)


def take_shard(values):
    size = values.shape[-1] // lax.axis_size("fsdp")
    return lax.dynamic_slice_in_dim(values, lax.axis_index("fsdp") * size, size, values.ndim - 1)


def shards(
    tokens,
    cotangent,
    ln1_gain,
    ln1_bias,
    qkv_weight,
    qv_bias,
    out_weight,
    out_bias,
    ln2_gain,
    ln2_bias,
    fc_weight,
    fc_bias,
    proj_weight,
    proj_bias,
):
    qkv_rows, qkv_parts, qkv_columns = qkv_weight.shape
    weight_qkv = gather_rows(qkv_weight.reshape(qkv_rows, qkv_parts * qkv_columns))
    width = weight_qkv.shape[0]
    weight_qkv = weight_qkv.reshape(width, qkv_parts, qkv_columns)
    vectors = (ln1_gain, ln1_bias, qv_bias[0], qv_bias[1], out_bias, ln2_gain, ln2_bias)
    vectors = vectors + (fc_bias, proj_bias)
    packed = lax.all_gather(jnp.concatenate(vectors), "fsdp", axis=0, tiled=False)
    full_vectors = []
    begin = 0
    for vector in vectors:
        full_vectors.append(packed[:, begin : begin + vector.shape[0]].reshape(-1))
        begin += vector.shape[0]
    gain_one, bias_one, bias_q, bias_v, bias_out, gain_two, bias_two = full_vectors[:7]
    bias_fc, bias_proj = full_vectors[7:]
    out_columns = out_weight.shape[0]
    hidden = fc_weight.shape[1]
    rest = jnp.concatenate([own_part(out_weight.T), own_part(fc_weight), own_part(proj_weight.T)], 1)
    rest = lax.all_gather(rest, ("fsdp", "ctx"), axis=0, tiled=True)
    weight_out = rest[:, :out_columns]
    weight_fc = rest[:, out_columns : out_columns + hidden]
    weight_proj = rest[:, out_columns + hidden :]
    inputs = tokens[0]
    upstream = cotangent[0]
    local_width = weight_qkv.shape[2]
    inputs_full = inputs.astype(jnp.float32)
    gain_one_f = gain_one.astype(jnp.float32)
    gain_two_f = gain_two.astype(jnp.float32)
    normed_one, inv_one = norm_forward(inputs_full)
    hidden_one = (normed_one * gain_one_f + bias_one.astype(jnp.float32)).astype(jnp.bfloat16)
    qkv_full = contract("td,dcf->ctf", hidden_one, weight_qkv)
    zero_row = jnp.zeros((local_width,), jnp.float32)
    bias_three = jnp.stack(
        [bias_q.astype(jnp.float32), zero_row, bias_v.astype(jnp.float32)]
    )
    qkv_low = (qkv_full + bias_three[:, None, :]).astype(jnp.bfloat16)
    spread = lax.all_to_all(qkv_low, "ctx", split_axis=2, concat_axis=1, tiled=True)
    length = spread.shape[1]
    per_device = spread.shape[2] // HD
    head_view = spread.reshape(3, length, per_device, HD).transpose(0, 2, 1, 3)
    heads_out, log_total = attend(head_view[0], head_view[1], head_view[2])
    heads_flat = heads_out.transpose(1, 0, 2).reshape(length, per_device * HD)
    heads_rows = lax.all_to_all(heads_flat, "ctx", split_axis=0, concat_axis=1, tiled=True)
    attn_part = contract("tf,df->td", heads_rows, weight_out)
    mid = (
        inputs_full
        + pair_sum(attn_part.astype(jnp.bfloat16))
        + bias_out.astype(jnp.float32)
    )
    normed_two, inv_two = norm_forward(mid)
    hidden_two = (normed_two * gain_two_f + bias_two.astype(jnp.float32)).astype(jnp.bfloat16)
    pre_act = contract("td,df->tf", hidden_two, weight_fc) + bias_fc.astype(jnp.float32)
    act_full, act_slope = gelu_parts(pre_act)
    act_low = act_full.astype(jnp.bfloat16)
    mlp_part = contract("tf,df->td", act_low, weight_proj)
    layer_out = (
        mid
        + pair_sum(mlp_part.astype(jnp.bfloat16))
        + bias_proj.astype(jnp.float32)
    ).astype(jnp.bfloat16)
    upstream_full = upstream.astype(jnp.float32)
    grad_proj_weight = contract("td,tf->df", upstream, act_low)
    grad_proj_bias = jnp.sum(upstream_full, axis=0)
    grad_pre = contract("td,df->tf", upstream, weight_proj) * act_slope
    grad_pre_low = grad_pre.astype(jnp.bfloat16)
    grad_fc_bias = jnp.sum(grad_pre, axis=0)
    grad_fc_weight = contract("td,tf->df", hidden_two, grad_pre_low)
    grad_hidden_two = pair_sum(
        contract("tf,df->td", grad_pre_low, weight_fc).astype(jnp.bfloat16)
    )
    grad_ln2_gain = jnp.sum(grad_hidden_two * normed_two, axis=0)
    grad_ln2_bias = jnp.sum(grad_hidden_two, axis=0)
    grad_mid = upstream_full + norm_backward(grad_hidden_two, normed_two, inv_two, gain_two_f)
    grad_mid_low = grad_mid.astype(jnp.bfloat16)
    grad_out_bias = jnp.sum(grad_mid, axis=0)
    grad_out_weight = contract("td,tf->df", grad_mid_low, heads_rows)
    grad_heads = contract("td,df->tf", grad_mid_low, weight_out).astype(jnp.bfloat16)
    block_grads = jnp.concatenate(
        [
            grad_out_weight.astype(jnp.bfloat16),
            grad_fc_weight.astype(jnp.bfloat16),
            grad_proj_weight.astype(jnp.bfloat16),
        ],
        axis=1,
    )
    grad_heads, block_grads = lax.optimization_barrier((grad_heads, block_grads))
    block_part = scatter_rows(block_grads)
    grad_spread = lax.all_to_all(grad_heads, "ctx", split_axis=1, concat_axis=0, tiled=True)
    grad_head_view = grad_spread.reshape(length, per_device, HD).transpose(1, 0, 2)
    grad_queries, grad_keys, grad_values = attend_back(
        head_view[0], head_view[1], head_view[2], heads_out, log_total, grad_head_view
    )
    grad_qkv = jnp.stack([grad_queries, grad_keys, grad_values]).astype(jnp.bfloat16)
    grad_qkv = grad_qkv.transpose(0, 2, 1, 3).reshape(3, length, per_device * HD)
    grad_local = lax.all_to_all(grad_qkv, "ctx", split_axis=1, concat_axis=2, tiled=True)
    grad_qv_bias = jnp.stack(
        [
            jnp.sum(grad_local[0].astype(jnp.float32), axis=0),
            jnp.sum(grad_local[2].astype(jnp.float32), axis=0),
        ]
    )
    grad_qkv_weight = contract("td,ctf->dcf", hidden_one, grad_local)
    grad_hidden_one = pair_sum(
        contract("ctf,dcf->td", grad_local, weight_qkv).astype(jnp.bfloat16)
    )
    grad_ln1_gain = jnp.sum(grad_hidden_one * normed_one, axis=0)
    grad_ln1_bias = jnp.sum(grad_hidden_one, axis=0)
    grad_input = (
        grad_mid + norm_backward(grad_hidden_one, normed_one, inv_one, gain_one_f)
    ).astype(jnp.bfloat16)
    flat_qkv = grad_qkv_weight.reshape(width, qkv_parts * qkv_columns).astype(jnp.bfloat16)
    flat_qkv, block_part = lax.optimization_barrier((flat_qkv, block_part))
    out_qkv = join_rows(scatter_rows(flat_qkv))
    block_sum = join_rows(block_part)
    sum_out = block_sum[:, :out_columns]
    sum_fc = block_sum[:, out_columns : out_columns + hidden]
    sum_proj = block_sum[:, out_columns + hidden :]
    small = (grad_ln1_gain, grad_ln1_bias, grad_qv_bias[0], grad_qv_bias[1], grad_out_bias)
    small = small + (grad_ln2_gain, grad_ln2_bias, grad_fc_bias, grad_proj_bias)
    small_low = jnp.concatenate(small).astype(jnp.bfloat16)
    spread_small = lax.all_gather(small_low, ("fsdp", "ctx"), axis=0, tiled=False)
    summed = jnp.sum(spread_small.astype(jnp.float32), axis=0)
    pieces = []
    begin = 0
    for vector in small:
        pieces.append(take_shard(summed[begin : begin + vector.shape[0]]))
        begin += vector.shape[0]
    final_grads = (
        pieces[0],
        pieces[1],
        out_qkv.astype(jnp.float32).reshape(qkv_rows, qkv_parts, qkv_columns),
        jnp.stack([pieces[2], pieces[3]]),
        sum_out.astype(jnp.float32).T,
        pieces[4],
        pieces[5],
        pieces[6],
        sum_fc.astype(jnp.float32),
        pieces[7],
        sum_proj.astype(jnp.float32).T,
        pieces[8],
    )
    return (
        layer_out[None],
        grad_input[None],
        final_grads[0],
        final_grads[1],
        final_grads[2],
        final_grads[3],
        final_grads[4],
        final_grads[5],
        final_grads[6],
        final_grads[7],
        final_grads[8],
        final_grads[9],
        final_grads[10],
        final_grads[11],
    )


def solution(mesh):
    return jax.shard_map(
        shards,
        mesh=mesh,
        in_specs=(
            P("fsdp", "ctx", None),
            P("fsdp", "ctx", None),
            P("fsdp"),
            P("fsdp"),
            P("fsdp", None, "tp"),
            P(None, ("tp", "fsdp")),
            P("tp", "fsdp"),
            P("fsdp"),
            P("fsdp"),
            P("fsdp"),
            P("fsdp", "tp"),
            P(("tp", "fsdp")),
            P("tp", "fsdp"),
            P("fsdp"),
        ),
        out_specs=(
            P("fsdp", "ctx", None),
            P("fsdp", "ctx", None),
            P("fsdp"),
            P("fsdp"),
            P("fsdp", None, "tp"),
            P(None, ("tp", "fsdp")),
            P("tp", "fsdp"),
            P("fsdp"),
            P("fsdp"),
            P("fsdp"),
            P("fsdp", "tp"),
            P(("tp", "fsdp")),
            P("tp", "fsdp"),
            P("fsdp"),
        ),
        check_vma=False,
    )
```

```python
import math

import jax
import jax.numpy as jnp
from jax import lax
from jax.sharding import PartitionSpec as P

HD = 64


EPSILON = 1e-05
GELU_COEF = math.sqrt(2.0 / math.pi)
MASK_FILL = -1e30


def contract(form, left, right):
    return jnp.einsum(form, left, right, preferred_element_type=jnp.float32)


def norm_forward(values):
    centre = jnp.mean(values, axis=-1, keepdims=True)
    centred = values - centre
    inverse = lax.rsqrt(jnp.mean(centred * centred, axis=-1, keepdims=True) + EPSILON)
    return (centred * inverse, inverse)


def norm_backward(upstream, normed, inverse, gain_full):
    scaled = upstream * gain_full
    first = jnp.mean(scaled, axis=-1, keepdims=True)
    second = jnp.mean(scaled * normed, axis=-1, keepdims=True)
    return inverse * (scaled - first - normed * second)


def gelu_parts(pre_act):
    cubic = pre_act * pre_act * pre_act
    tangent = jnp.tanh(GELU_COEF * (pre_act + 0.044715 * cubic))
    value_out = 0.5 * pre_act * (1.0 + tangent)
    slope_out = 0.5 * (1.0 + tangent) + 0.5 * pre_act * (1.0 - tangent * tangent) * GELU_COEF * (
        1.0 + 3.0 * 0.044715 * pre_act * pre_act
    )
    return (value_out, slope_out)


def causal_scores(query_block, key_heads, start_row):
    block_rows = query_block.shape[1]
    length = key_heads.shape[1]
    score_scale = query_block.shape[2] ** (-0.5)
    scores = contract("gqe,gke->gqk", query_block, key_heads) * score_scale
    query_pos = start_row + jnp.arange(block_rows, dtype=jnp.int32)
    key_pos = jnp.arange(length, dtype=jnp.int32)
    allowed = key_pos[None, :] <= query_pos[:, None]
    return jnp.where(allowed[None], scores, MASK_FILL)


def attend(query_heads, key_heads, value_heads):
    groups, length, depth = query_heads.shape
    block_rows = min(512, length)
    block_count = length // block_rows

    def one_block(block_index):
        start_row = block_index * block_rows
        query_block = lax.dynamic_slice_in_dim(query_heads, start_row, block_rows, 1)
        scores = causal_scores(query_block, key_heads, start_row)
        row_max = jnp.max(scores, axis=-1, keepdims=True)
        log_total = row_max[..., 0] + jnp.log(jnp.sum(jnp.exp(scores - row_max), axis=-1))
        soft_weights = jnp.exp(scores - log_total[..., None]).astype(jnp.bfloat16)
        block_out = contract("gqk,gke->gqe", soft_weights, value_heads).astype(jnp.bfloat16)
        return (block_out, log_total)

    outputs, totals = lax.map(one_block, jnp.arange(block_count, dtype=jnp.int32))
    outputs = outputs.transpose(1, 0, 2, 3).reshape(groups, length, depth)
    totals = totals.transpose(1, 0, 2).reshape(groups, length)
    return (outputs, totals)


def attend_back(query_heads, key_heads, value_heads, output_heads, log_total, grad_heads):
    groups, length, depth = query_heads.shape
    block_rows = min(512, length)
    block_count = length // block_rows
    score_scale = depth ** (-0.5)

    def one_block(carried, block_index):
        grad_keys, grad_values = carried
        start_row = block_index * block_rows
        query_block = lax.dynamic_slice_in_dim(query_heads, start_row, block_rows, 1)
        output_block = lax.dynamic_slice_in_dim(output_heads, start_row, block_rows, 1)
        grad_block = lax.dynamic_slice_in_dim(grad_heads, start_row, block_rows, 1)
        total_block = lax.dynamic_slice_in_dim(log_total, start_row, block_rows, 1)
        scores = causal_scores(query_block, key_heads, start_row)
        soft_full = jnp.exp(scores - total_block[..., None])
        soft_low = soft_full.astype(jnp.bfloat16)
        grad_values = grad_values + contract("gqk,gqe->gke", soft_low, grad_block)
        grad_soft = contract("gqe,gke->gqk", grad_block, value_heads)
        diagonal = jnp.sum(
            grad_block.astype(jnp.float32) * output_block.astype(jnp.float32), axis=-1
        )
        grad_scores = (soft_full * (grad_soft - diagonal[..., None]) * score_scale).astype(
            jnp.bfloat16
        )
        grad_query = contract("gqk,gke->gqe", grad_scores, key_heads)
        grad_keys = grad_keys + contract("gqk,gqe->gke", grad_scores, query_block)
        return ((grad_keys, grad_values), grad_query)

    zero_heads = jnp.zeros((groups, length, depth), jnp.float32)
    (grad_keys, grad_values), grad_queries = lax.scan(
        one_block, (zero_heads, zero_heads), jnp.arange(block_count, dtype=jnp.int32)
    )
    grad_queries = grad_queries.transpose(1, 0, 2, 3).reshape(groups, length, depth)
    return (grad_queries, grad_keys, grad_values)


def own_part(values):
    rows = values.shape[0] // lax.axis_size("ctx")
    return lax.dynamic_slice_in_dim(values, lax.axis_index("ctx") * rows, rows, 0)


def scatter_rows(grad):
    return lax.psum_scatter(
        grad.astype(jnp.bfloat16), ("fsdp", "ctx"), scatter_dimension=0, tiled=True
    )


def join_rows(part):
    members = lax.axis_size("ctx")
    if members & (members - 1):
        return lax.all_gather(part, "ctx", axis=0, tiled=True)
    place = lax.axis_index("ctx")
    rows, columns = part.shape
    held = part[None]
    step = members // 2
    while step:
        other = lax.ppermute(held, "ctx", [(i, i ^ step) for i in range(members)])
        upper = (place // step) % 2 == 1
        first = jnp.where(upper, other, held)
        second = jnp.where(upper, held, other)
        held = jnp.stack([first, second], axis=1).reshape(-1, rows, columns)
        step //= 2
    return held.reshape(members * rows, columns)


def gather_hops(shard):
    size = lax.axis_size("fsdp")
    place = lax.axis_index("fsdp")
    part = own_part(shard)
    part = part.reshape(part.shape[0], -1)
    rows, columns = part.shape
    whole = jnp.zeros((size, rows, columns), part.dtype)
    whole = lax.dynamic_update_slice_in_dim(whole, part[None], place, 0)
    for hop in range(1, size):
        other = lax.ppermute(part, "fsdp", [(i, (i + hop) % size) for i in range(size)])
        whole = lax.dynamic_update_slice_in_dim(whole, other[None], (place - hop) % size, 0)
    joined = join_rows(whole.reshape(size * rows, columns))
    members = lax.axis_size("ctx")
    joined = joined.reshape(members, size, rows, columns).transpose(1, 0, 2, 3)
    return joined.reshape(size * members * rows, columns)


def scatter_hops(grad):
    size = lax.axis_size("fsdp")
    members = lax.axis_size("ctx")
    if members & (members - 1):
        return scatter_rows(grad)
    place = lax.axis_index("fsdp")
    member = lax.axis_index("ctx")
    rows = grad.shape[0] // (size * members)
    columns = grad.shape[1]
    held = grad.astype(jnp.bfloat16)
    step = 1
    while step < members:
        held = held.reshape(-1, 2, rows, columns)
        bit = (member // step) % 2
        kept = lax.dynamic_index_in_dim(held, bit, 1, keepdims=False)
        sent = lax.dynamic_index_in_dim(held, 1 - bit, 1, keepdims=False)
        other = lax.ppermute(sent, "ctx", [(i, i ^ step) for i in range(members)])
        held = (kept.astype(jnp.float32) + other.astype(jnp.float32)).astype(jnp.bfloat16)
        step *= 2
    held = held.reshape(size, rows, columns)
    total = lax.dynamic_index_in_dim(held, place, 0, keepdims=False).astype(jnp.float32)
    for hop in range(1, size):
        sent = lax.dynamic_index_in_dim(held, (place + hop) % size, 0, keepdims=False)
        other = lax.ppermute(sent, "fsdp", [(i, (i + hop) % size) for i in range(size)])
        total = total + other.astype(jnp.float32)
    return total.astype(jnp.bfloat16)


def sum_hops(values):
    for axis in ("ctx", "fsdp"):
        size = lax.axis_size(axis)
        if size & (size - 1):
            values = lax.psum(values, axis)
            continue
        step = 1
        while step < size:
            values = values + lax.ppermute(values, axis, [(i, i ^ step) for i in range(size)])
            step *= 2
    return values


def pair_sum(values):
    if lax.axis_size("tp") == 2:
        other = lax.ppermute(values, "tp", [(0, 1), (1, 0)])
        return values.astype(jnp.float32) + other.astype(jnp.float32)
    return lax.psum(values, "tp").astype(jnp.float32)


def take_shard(values):
    size = values.shape[-1] // lax.axis_size("fsdp")
    return lax.dynamic_slice_in_dim(values, lax.axis_index("fsdp") * size, size, values.ndim - 1)


def shards(
    tokens,
    cotangent,
    ln1_gain,
    ln1_bias,
    qkv_weight,
    qv_bias,
    out_weight,
    out_bias,
    ln2_gain,
    ln2_bias,
    fc_weight,
    fc_bias,
    proj_weight,
    proj_bias,
):
    qkv_rows, qkv_parts, qkv_columns = qkv_weight.shape
    weight_qkv = gather_hops(qkv_weight)
    vectors = (ln1_gain, ln1_bias, qv_bias[0], qv_bias[1], out_bias, ln2_gain, ln2_bias)
    vectors = vectors + (fc_bias, proj_bias)
    packed = lax.all_gather(jnp.concatenate(vectors), "fsdp", axis=0, tiled=False)
    full_vectors = []
    begin = 0
    for vector in vectors:
        full_vectors.append(packed[:, begin : begin + vector.shape[0]].reshape(-1))
        begin += vector.shape[0]
    gain_one, bias_one, bias_q, bias_v, bias_out, gain_two, bias_two = full_vectors[:7]
    bias_fc, bias_proj = full_vectors[7:]
    out_columns = out_weight.shape[0]
    hidden = fc_weight.shape[1]
    rest = jnp.concatenate([own_part(out_weight.T), own_part(fc_weight), own_part(proj_weight.T)], 1)
    rest = lax.all_gather(rest, ("fsdp", "ctx"), axis=0, tiled=True)
    weight_out = rest[:, :out_columns]
    weight_fc = rest[:, out_columns : out_columns + hidden]
    weight_proj = rest[:, out_columns + hidden :]
    inputs = tokens[0]
    upstream = cotangent[0]
    local_width = qkv_columns
    inputs_full = inputs.astype(jnp.float32)
    gain_one_f = gain_one.astype(jnp.float32)
    gain_two_f = gain_two.astype(jnp.float32)
    normed_one, inv_one = norm_forward(inputs_full)
    hidden_one = (normed_one * gain_one_f + bias_one.astype(jnp.float32)).astype(jnp.bfloat16)
    qkv_full = contract("td,df->tf", hidden_one, weight_qkv)
    qkv_full = qkv_full.reshape(-1, qkv_parts, qkv_columns).transpose(1, 0, 2)
    zero_row = jnp.zeros((local_width,), jnp.float32)
    bias_three = jnp.stack(
        [bias_q.astype(jnp.float32), zero_row, bias_v.astype(jnp.float32)]
    )
    qkv_low = (qkv_full + bias_three[:, None, :]).astype(jnp.bfloat16)
    spread = lax.all_to_all(qkv_low, "ctx", split_axis=2, concat_axis=1, tiled=True)
    length = spread.shape[1]
    per_device = spread.shape[2] // HD
    head_view = spread.reshape(3, length, per_device, HD).transpose(0, 2, 1, 3)
    heads_out, log_total = attend(head_view[0], head_view[1], head_view[2])
    heads_flat = heads_out.transpose(1, 0, 2).reshape(length, per_device * HD)
    heads_rows = lax.all_to_all(heads_flat, "ctx", split_axis=0, concat_axis=1, tiled=True)
    attn_part = contract("tf,df->td", heads_rows, weight_out)
    mid = (
        inputs_full
        + pair_sum(attn_part.astype(jnp.bfloat16))
        + bias_out.astype(jnp.float32)
    )
    normed_two, inv_two = norm_forward(mid)
    hidden_two = (normed_two * gain_two_f + bias_two.astype(jnp.float32)).astype(jnp.bfloat16)
    pre_act = contract("td,df->tf", hidden_two, weight_fc) + bias_fc.astype(jnp.float32)
    act_full, act_slope = gelu_parts(pre_act)
    act_low = act_full.astype(jnp.bfloat16)
    mlp_part = contract("tf,df->td", act_low, weight_proj)
    layer_out = (
        mid
        + pair_sum(mlp_part.astype(jnp.bfloat16))
        + bias_proj.astype(jnp.float32)
    ).astype(jnp.bfloat16)
    upstream_full = upstream.astype(jnp.float32)
    grad_proj_weight = contract("td,tf->df", upstream, act_low)
    grad_proj_bias = jnp.sum(upstream_full, axis=0)
    grad_pre = contract("td,df->tf", upstream, weight_proj) * act_slope
    grad_pre_low = grad_pre.astype(jnp.bfloat16)
    grad_fc_bias = jnp.sum(grad_pre, axis=0)
    grad_fc_weight = contract("td,tf->df", hidden_two, grad_pre_low)
    grad_hidden_two = pair_sum(
        contract("tf,df->td", grad_pre_low, weight_fc).astype(jnp.bfloat16)
    )
    grad_ln2_gain = jnp.sum(grad_hidden_two * normed_two, axis=0)
    grad_ln2_bias = jnp.sum(grad_hidden_two, axis=0)
    grad_mid = upstream_full + norm_backward(grad_hidden_two, normed_two, inv_two, gain_two_f)
    grad_mid_low = grad_mid.astype(jnp.bfloat16)
    grad_out_bias = jnp.sum(grad_mid, axis=0)
    grad_out_weight = contract("td,tf->df", grad_mid_low, heads_rows)
    grad_heads = contract("td,df->tf", grad_mid_low, weight_out).astype(jnp.bfloat16)
    block_grads = jnp.concatenate(
        [
            grad_out_weight.astype(jnp.bfloat16),
            grad_fc_weight.astype(jnp.bfloat16),
            grad_proj_weight.astype(jnp.bfloat16),
        ],
        axis=1,
    )
    grad_heads, block_grads = lax.optimization_barrier((grad_heads, block_grads))
    block_part = scatter_rows(block_grads)
    grad_spread = lax.all_to_all(grad_heads, "ctx", split_axis=1, concat_axis=0, tiled=True)
    grad_head_view = grad_spread.reshape(length, per_device, HD).transpose(1, 0, 2)
    grad_queries, grad_keys, grad_values = attend_back(
        head_view[0], head_view[1], head_view[2], heads_out, log_total, grad_head_view
    )
    grad_qkv = jnp.stack([grad_queries, grad_keys, grad_values]).astype(jnp.bfloat16)
    grad_qkv = grad_qkv.transpose(0, 2, 1, 3).reshape(3, length, per_device * HD)
    grad_local = lax.all_to_all(grad_qkv, "ctx", split_axis=1, concat_axis=2, tiled=True)
    grad_qv_bias = jnp.stack(
        [
            jnp.sum(grad_local[0].astype(jnp.float32), axis=0),
            jnp.sum(grad_local[2].astype(jnp.float32), axis=0),
        ]
    )
    grad_rows = jnp.concatenate([grad_local[c] for c in range(qkv_parts)], axis=1)
    grad_qkv_weight = contract("td,tf->df", hidden_one, grad_rows)
    grad_hidden_one = pair_sum(
        contract("tf,df->td", grad_rows, weight_qkv).astype(jnp.bfloat16)
    )
    grad_ln1_gain = jnp.sum(grad_hidden_one * normed_one, axis=0)
    grad_ln1_bias = jnp.sum(grad_hidden_one, axis=0)
    grad_input = (
        grad_mid + norm_backward(grad_hidden_one, normed_one, inv_one, gain_one_f)
    ).astype(jnp.bfloat16)
    out_qkv = join_rows(scatter_hops(grad_qkv_weight))
    block_sum = join_rows(block_part)
    sum_out = block_sum[:, :out_columns]
    sum_fc = block_sum[:, out_columns : out_columns + hidden]
    sum_proj = block_sum[:, out_columns + hidden :]
    small = (grad_ln1_gain, grad_ln1_bias, grad_qv_bias[0], grad_qv_bias[1], grad_out_bias)
    small = small + (grad_ln2_gain, grad_ln2_bias, grad_fc_bias, grad_proj_bias)
    summed = sum_hops(jnp.concatenate(small))
    pieces = []
    begin = 0
    for vector in small:
        pieces.append(take_shard(summed[begin : begin + vector.shape[0]]))
        begin += vector.shape[0]
    final_grads = (
        pieces[0],
        pieces[1],
        out_qkv.astype(jnp.float32).reshape(qkv_rows, qkv_parts, qkv_columns),
        jnp.stack([pieces[2], pieces[3]]),
        sum_out.astype(jnp.float32).T,
        pieces[4],
        pieces[5],
        pieces[6],
        sum_fc.astype(jnp.float32),
        pieces[7],
        sum_proj.astype(jnp.float32).T,
        pieces[8],
    )
    return (
        layer_out[None],
        grad_input[None],
        final_grads[0],
        final_grads[1],
        final_grads[2],
        final_grads[3],
        final_grads[4],
        final_grads[5],
        final_grads[6],
        final_grads[7],
        final_grads[8],
        final_grads[9],
        final_grads[10],
        final_grads[11],
    )


def solution(mesh):
    return jax.shard_map(
        shards,
        mesh=mesh,
        in_specs=(
            P("fsdp", "ctx", None),
            P("fsdp", "ctx", None),
            P("fsdp"),
            P("fsdp"),
            P("fsdp", None, "tp"),
            P(None, ("tp", "fsdp")),
            P("tp", "fsdp"),
            P("fsdp"),
            P("fsdp"),
            P("fsdp"),
            P("fsdp", "tp"),
            P(("tp", "fsdp")),
            P("tp", "fsdp"),
            P("fsdp"),
        ),
        out_specs=(
            P("fsdp", "ctx", None),
            P("fsdp", "ctx", None),
            P("fsdp"),
            P("fsdp"),
            P("fsdp", None, "tp"),
            P(None, ("tp", "fsdp")),
            P("tp", "fsdp"),
            P("fsdp"),
            P("fsdp"),
            P("fsdp"),
            P("fsdp", "tp"),
            P(("tp", "fsdp")),
            P("tp", "fsdp"),
            P("fsdp"),
        ),
        check_vma=False,
    )
```

```python
import math

import jax
import jax.numpy as jnp
from jax import lax
from jax.sharding import PartitionSpec as P

HD = 64


EPSILON = 1e-05
GELU_COEF = math.sqrt(2.0 / math.pi)
MASK_FILL = -1e30


def contract(form, left, right):
    return jnp.einsum(form, left, right, preferred_element_type=jnp.float32)


def norm_forward(values):
    centre = jnp.mean(values, axis=-1, keepdims=True)
    centred = values - centre
    inverse = lax.rsqrt(jnp.mean(centred * centred, axis=-1, keepdims=True) + EPSILON)
    return (centred * inverse, inverse)


def norm_backward(upstream, normed, inverse, gain_full):
    scaled = upstream * gain_full
    first = jnp.mean(scaled, axis=-1, keepdims=True)
    second = jnp.mean(scaled * normed, axis=-1, keepdims=True)
    return inverse * (scaled - first - normed * second)


def gelu_parts(pre_act):
    cubic = pre_act * pre_act * pre_act
    tangent = jnp.tanh(GELU_COEF * (pre_act + 0.044715 * cubic))
    value_out = 0.5 * pre_act * (1.0 + tangent)
    slope_out = 0.5 * (1.0 + tangent) + 0.5 * pre_act * (1.0 - tangent * tangent) * GELU_COEF * (
        1.0 + 3.0 * 0.044715 * pre_act * pre_act
    )
    return (value_out, slope_out)


def causal_scores(query_block, key_heads, start_row):
    block_rows = query_block.shape[1]
    length = key_heads.shape[1]
    score_scale = query_block.shape[2] ** (-0.5)
    scores = contract("gqe,gke->gqk", query_block, key_heads) * score_scale
    query_pos = start_row + jnp.arange(block_rows, dtype=jnp.int32)
    key_pos = jnp.arange(length, dtype=jnp.int32)
    allowed = key_pos[None, :] <= query_pos[:, None]
    return jnp.where(allowed[None], scores, MASK_FILL)


def attend(query_heads, key_heads, value_heads):
    groups, length, depth = query_heads.shape
    block_rows = min(512, length)
    block_count = length // block_rows

    def one_block(block_index):
        start_row = block_index * block_rows
        query_block = lax.dynamic_slice_in_dim(query_heads, start_row, block_rows, 1)
        scores = causal_scores(query_block, key_heads, start_row)
        row_max = jnp.max(scores, axis=-1, keepdims=True)
        log_total = row_max[..., 0] + jnp.log(jnp.sum(jnp.exp(scores - row_max), axis=-1))
        soft_weights = jnp.exp(scores - log_total[..., None]).astype(jnp.bfloat16)
        block_out = contract("gqk,gke->gqe", soft_weights, value_heads).astype(jnp.bfloat16)
        return (block_out, log_total)

    outputs, totals = lax.map(one_block, jnp.arange(block_count, dtype=jnp.int32))
    outputs = outputs.transpose(1, 0, 2, 3).reshape(groups, length, depth)
    totals = totals.transpose(1, 0, 2).reshape(groups, length)
    return (outputs, totals)


def attend_back(query_heads, key_heads, value_heads, output_heads, log_total, grad_heads):
    groups, length, depth = query_heads.shape
    block_rows = min(512, length)
    block_count = length // block_rows
    score_scale = depth ** (-0.5)

    def one_block(carried, block_index):
        grad_keys, grad_values = carried
        start_row = block_index * block_rows
        query_block = lax.dynamic_slice_in_dim(query_heads, start_row, block_rows, 1)
        output_block = lax.dynamic_slice_in_dim(output_heads, start_row, block_rows, 1)
        grad_block = lax.dynamic_slice_in_dim(grad_heads, start_row, block_rows, 1)
        total_block = lax.dynamic_slice_in_dim(log_total, start_row, block_rows, 1)
        scores = causal_scores(query_block, key_heads, start_row)
        soft_full = jnp.exp(scores - total_block[..., None])
        soft_low = soft_full.astype(jnp.bfloat16)
        grad_values = grad_values + contract("gqk,gqe->gke", soft_low, grad_block)
        grad_soft = contract("gqe,gke->gqk", grad_block, value_heads)
        diagonal = jnp.sum(
            grad_block.astype(jnp.float32) * output_block.astype(jnp.float32), axis=-1
        )
        grad_scores = (soft_full * (grad_soft - diagonal[..., None]) * score_scale).astype(
            jnp.bfloat16
        )
        grad_query = contract("gqk,gke->gqe", grad_scores, key_heads)
        grad_keys = grad_keys + contract("gqk,gqe->gke", grad_scores, query_block)
        return ((grad_keys, grad_values), grad_query)

    zero_heads = jnp.zeros((groups, length, depth), jnp.float32)
    (grad_keys, grad_values), grad_queries = lax.scan(
        one_block, (zero_heads, zero_heads), jnp.arange(block_count, dtype=jnp.int32)
    )
    grad_queries = grad_queries.transpose(1, 0, 2, 3).reshape(groups, length, depth)
    return (grad_queries, grad_keys, grad_values)


def own_part(values):
    rows = values.shape[0] // lax.axis_size("ctx")
    return lax.dynamic_slice_in_dim(values, lax.axis_index("ctx") * rows, rows, 0)


def scatter_rows(grad):
    return lax.psum_scatter(
        grad.astype(jnp.bfloat16), ("fsdp", "ctx"), scatter_dimension=0, tiled=True
    )


def join_rows(part):
    members = lax.axis_size("ctx")
    if members & (members - 1):
        return lax.all_gather(part, "ctx", axis=0, tiled=True)
    place = lax.axis_index("ctx")
    rows, columns = part.shape
    held = part[None]
    step = members // 2
    while step:
        other = lax.ppermute(held, "ctx", [(i, i ^ step) for i in range(members)])
        upper = (place // step) % 2 == 1
        first = jnp.where(upper, other, held)
        second = jnp.where(upper, held, other)
        held = jnp.stack([first, second], axis=1).reshape(-1, rows, columns)
        step //= 2
    return held.reshape(members * rows, columns)


def gather_hops(shard):
    size = lax.axis_size("fsdp")
    place = lax.axis_index("fsdp")
    part = own_part(shard)
    part = part.reshape(part.shape[0], -1)
    rows, columns = part.shape
    whole = jnp.zeros((size, rows, columns), part.dtype)
    whole = lax.dynamic_update_slice_in_dim(whole, part[None], place, 0)
    for hop in range(1, size):
        other = lax.ppermute(part, "fsdp", [(i, (i + hop) % size) for i in range(size)])
        whole = lax.dynamic_update_slice_in_dim(whole, other[None], (place - hop) % size, 0)
    joined = join_rows(whole.reshape(size * rows, columns))
    members = lax.axis_size("ctx")
    joined = joined.reshape(members, size, rows, columns).transpose(1, 0, 2, 3)
    return joined.reshape(size * members * rows, columns)


def scatter_hops(grad):
    size = lax.axis_size("fsdp")
    members = lax.axis_size("ctx")
    if members & (members - 1):
        return scatter_rows(grad)
    place = lax.axis_index("fsdp")
    member = lax.axis_index("ctx")
    rows = grad.shape[0] // (size * members)
    columns = grad.shape[1]
    held = grad.astype(jnp.bfloat16)
    step = 1
    while step < members:
        held = held.reshape(-1, 2, rows, columns)
        bit = (member // step) % 2
        kept = lax.dynamic_index_in_dim(held, bit, 1, keepdims=False)
        sent = lax.dynamic_index_in_dim(held, 1 - bit, 1, keepdims=False)
        other = lax.ppermute(sent, "ctx", [(i, i ^ step) for i in range(members)])
        held = (kept.astype(jnp.float32) + other.astype(jnp.float32)).astype(jnp.bfloat16)
        step *= 2
    held = held.reshape(size, rows, columns)
    total = lax.dynamic_index_in_dim(held, place, 0, keepdims=False).astype(jnp.float32)
    for hop in range(1, size):
        sent = lax.dynamic_index_in_dim(held, (place + hop) % size, 0, keepdims=False)
        other = lax.ppermute(sent, "fsdp", [(i, (i + hop) % size) for i in range(size)])
        total = total + other.astype(jnp.float32)
    return total.astype(jnp.bfloat16)


def sum_hops(values):
    for axis in ("ctx", "fsdp"):
        size = lax.axis_size(axis)
        if size & (size - 1):
            values = lax.psum(values, axis)
            continue
        step = 1
        while step < size:
            values = values + lax.ppermute(values, axis, [(i, i ^ step) for i in range(size)])
            step *= 2
    return values


def pair_sum(values):
    if lax.axis_size("tp") == 2:
        other = lax.ppermute(values, "tp", [(0, 1), (1, 0)])
        return values.astype(jnp.float32) + other.astype(jnp.float32)
    return lax.psum(values, "tp").astype(jnp.float32)


def take_shard(values):
    size = values.shape[-1] // lax.axis_size("fsdp")
    return lax.dynamic_slice_in_dim(values, lax.axis_index("fsdp") * size, size, values.ndim - 1)


def shards(
    tokens,
    cotangent,
    ln1_gain,
    ln1_bias,
    qkv_weight,
    qv_bias,
    out_weight,
    out_bias,
    ln2_gain,
    ln2_bias,
    fc_weight,
    fc_bias,
    proj_weight,
    proj_bias,
):
    qkv_rows, qkv_parts, qkv_columns = qkv_weight.shape
    weight_qkv = gather_hops(qkv_weight)
    vectors = (ln1_gain, ln1_bias, qv_bias[0], qv_bias[1], out_bias, ln2_gain, ln2_bias)
    vectors = vectors + (fc_bias, proj_bias)
    own = jnp.concatenate(vectors)[None]
    size = lax.axis_size("fsdp")
    place = lax.axis_index("fsdp")
    packed = jnp.zeros((size, own.shape[1]), own.dtype)
    packed = lax.dynamic_update_slice_in_dim(packed, own, place, 0)
    for hop in range(1, size):
        other = lax.ppermute(own, "fsdp", [(i, (i + hop) % size) for i in range(size)])
        packed = lax.dynamic_update_slice_in_dim(packed, other, (place - hop) % size, 0)
    full_vectors = []
    begin = 0
    for vector in vectors:
        full_vectors.append(packed[:, begin : begin + vector.shape[0]].reshape(-1))
        begin += vector.shape[0]
    gain_one, bias_one, bias_q, bias_v, bias_out, gain_two, bias_two = full_vectors[:7]
    bias_fc, bias_proj = full_vectors[7:]
    out_columns = out_weight.shape[0]
    hidden = fc_weight.shape[1]
    rest = jnp.concatenate([own_part(out_weight.T), own_part(fc_weight), own_part(proj_weight.T)], 1)
    rest = lax.all_gather(rest, ("fsdp", "ctx"), axis=0, tiled=True)
    weight_out = rest[:, :out_columns]
    weight_fc = rest[:, out_columns : out_columns + hidden]
    weight_proj = rest[:, out_columns + hidden :]
    inputs = tokens[0]
    upstream = cotangent[0]
    local_width = qkv_columns
    inputs_full = inputs.astype(jnp.float32)
    gain_one_f = gain_one.astype(jnp.float32)
    gain_two_f = gain_two.astype(jnp.float32)
    normed_one, inv_one = norm_forward(inputs_full)
    hidden_one = (normed_one * gain_one_f + bias_one.astype(jnp.float32)).astype(jnp.bfloat16)
    qkv_full = contract("td,df->tf", hidden_one, weight_qkv)
    qkv_full = qkv_full.reshape(-1, qkv_parts, qkv_columns).transpose(1, 0, 2)
    zero_row = jnp.zeros((local_width,), jnp.float32)
    bias_three = jnp.stack(
        [bias_q.astype(jnp.float32), zero_row, bias_v.astype(jnp.float32)]
    )
    qkv_low = (qkv_full + bias_three[:, None, :]).astype(jnp.bfloat16)
    spread = lax.all_to_all(qkv_low, "ctx", split_axis=2, concat_axis=1, tiled=True)
    length = spread.shape[1]
    per_device = spread.shape[2] // HD
    head_view = spread.reshape(3, length, per_device, HD).transpose(0, 2, 1, 3)
    heads_out, log_total = attend(head_view[0], head_view[1], head_view[2])
    heads_flat = heads_out.transpose(1, 0, 2).reshape(length, per_device * HD)
    heads_rows = lax.all_to_all(heads_flat, "ctx", split_axis=0, concat_axis=1, tiled=True)
    attn_part = contract("tf,df->td", heads_rows, weight_out)
    mid = (
        inputs_full
        + pair_sum(attn_part.astype(jnp.bfloat16))
        + bias_out.astype(jnp.float32)
    )
    normed_two, inv_two = norm_forward(mid)
    hidden_two = (normed_two * gain_two_f + bias_two.astype(jnp.float32)).astype(jnp.bfloat16)
    pre_act = contract("td,df->tf", hidden_two, weight_fc) + bias_fc.astype(jnp.float32)
    act_full, act_slope = gelu_parts(pre_act)
    act_low = act_full.astype(jnp.bfloat16)
    mlp_part = contract("tf,df->td", act_low, weight_proj)
    layer_out = (
        mid
        + pair_sum(mlp_part.astype(jnp.bfloat16))
        + bias_proj.astype(jnp.float32)
    ).astype(jnp.bfloat16)
    upstream_full = upstream.astype(jnp.float32)
    grad_proj_weight = contract("td,tf->df", upstream, act_low)
    grad_proj_bias = jnp.sum(upstream_full, axis=0)
    grad_pre = contract("td,df->tf", upstream, weight_proj) * act_slope
    grad_pre_low = grad_pre.astype(jnp.bfloat16)
    grad_fc_bias = jnp.sum(grad_pre, axis=0)
    grad_fc_weight = contract("td,tf->df", hidden_two, grad_pre_low)
    grad_hidden_two = pair_sum(
        contract("tf,df->td", grad_pre_low, weight_fc).astype(jnp.bfloat16)
    )
    grad_ln2_gain = jnp.sum(grad_hidden_two * normed_two, axis=0)
    grad_ln2_bias = jnp.sum(grad_hidden_two, axis=0)
    grad_mid = upstream_full + norm_backward(grad_hidden_two, normed_two, inv_two, gain_two_f)
    grad_mid_low = grad_mid.astype(jnp.bfloat16)
    grad_out_bias = jnp.sum(grad_mid, axis=0)
    grad_out_weight = contract("td,tf->df", grad_mid_low, heads_rows)
    grad_heads = contract("td,df->tf", grad_mid_low, weight_out).astype(jnp.bfloat16)
    block_grads = jnp.concatenate(
        [
            grad_out_weight.astype(jnp.bfloat16),
            grad_fc_weight.astype(jnp.bfloat16),
            grad_proj_weight.astype(jnp.bfloat16),
        ],
        axis=1,
    )
    grad_heads, block_grads = lax.optimization_barrier((grad_heads, block_grads))
    block_part = scatter_rows(block_grads)
    grad_spread = lax.all_to_all(grad_heads, "ctx", split_axis=1, concat_axis=0, tiled=True)
    grad_head_view = grad_spread.reshape(length, per_device, HD).transpose(1, 0, 2)
    grad_queries, grad_keys, grad_values = attend_back(
        head_view[0], head_view[1], head_view[2], heads_out, log_total, grad_head_view
    )
    grad_qkv = jnp.stack([grad_queries, grad_keys, grad_values]).astype(jnp.bfloat16)
    grad_qkv = grad_qkv.transpose(0, 2, 1, 3).reshape(3, length, per_device * HD)
    grad_local = lax.all_to_all(grad_qkv, "ctx", split_axis=1, concat_axis=2, tiled=True)
    grad_qv_bias = jnp.stack(
        [
            jnp.sum(grad_local[0].astype(jnp.float32), axis=0),
            jnp.sum(grad_local[2].astype(jnp.float32), axis=0),
        ]
    )
    grad_rows = jnp.concatenate([grad_local[c] for c in range(qkv_parts)], axis=1)
    grad_qkv_weight = contract("td,tf->df", hidden_one, grad_rows)
    grad_hidden_one = pair_sum(
        contract("tf,df->td", grad_rows, weight_qkv).astype(jnp.bfloat16)
    )
    grad_ln1_gain = jnp.sum(grad_hidden_one * normed_one, axis=0)
    grad_ln1_bias = jnp.sum(grad_hidden_one, axis=0)
    grad_input = (
        grad_mid + norm_backward(grad_hidden_one, normed_one, inv_one, gain_one_f)
    ).astype(jnp.bfloat16)
    out_qkv = join_rows(scatter_hops(grad_qkv_weight))
    block_sum = join_rows(block_part)
    sum_out = block_sum[:, :out_columns]
    sum_fc = block_sum[:, out_columns : out_columns + hidden]
    sum_proj = block_sum[:, out_columns + hidden :]
    small = (grad_ln1_gain, grad_ln1_bias, grad_qv_bias[0], grad_qv_bias[1], grad_out_bias)
    small = small + (grad_ln2_gain, grad_ln2_bias, grad_fc_bias, grad_proj_bias)
    summed = sum_hops(jnp.concatenate(small))
    pieces = []
    begin = 0
    for vector in small:
        pieces.append(take_shard(summed[begin : begin + vector.shape[0]]))
        begin += vector.shape[0]
    final_grads = (
        pieces[0],
        pieces[1],
        out_qkv.astype(jnp.float32).reshape(qkv_rows, qkv_parts, qkv_columns),
        jnp.stack([pieces[2], pieces[3]]),
        sum_out.astype(jnp.float32).T,
        pieces[4],
        pieces[5],
        pieces[6],
        sum_fc.astype(jnp.float32),
        pieces[7],
        sum_proj.astype(jnp.float32).T,
        pieces[8],
    )
    return (
        layer_out[None],
        grad_input[None],
        final_grads[0],
        final_grads[1],
        final_grads[2],
        final_grads[3],
        final_grads[4],
        final_grads[5],
        final_grads[6],
        final_grads[7],
        final_grads[8],
        final_grads[9],
        final_grads[10],
        final_grads[11],
    )


def solution(mesh):
    return jax.shard_map(
        shards,
        mesh=mesh,
        in_specs=(
            P("fsdp", "ctx", None),
            P("fsdp", "ctx", None),
            P("fsdp"),
            P("fsdp"),
            P("fsdp", None, "tp"),
            P(None, ("tp", "fsdp")),
            P("tp", "fsdp"),
            P("fsdp"),
            P("fsdp"),
            P("fsdp"),
            P("fsdp", "tp"),
            P(("tp", "fsdp")),
            P("tp", "fsdp"),
            P("fsdp"),
        ),
        out_specs=(
            P("fsdp", "ctx", None),
            P("fsdp", "ctx", None),
            P("fsdp"),
            P("fsdp"),
            P("fsdp", None, "tp"),
            P(None, ("tp", "fsdp")),
            P("tp", "fsdp"),
            P("fsdp"),
            P("fsdp"),
            P("fsdp"),
            P("fsdp", "tp"),
            P(("tp", "fsdp")),
            P("tp", "fsdp"),
            P("fsdp"),
        ),
        check_vma=False,
    )
```
